32 devices in a mesh: tiles: 2 (over y), disp: 4 (over z), rows: 2 (over x), cols: 2 (over core).
Axes of the slice: x: 2, y: 2, z: 4, core: 2. Of those that a mesh axis runs over, the one named last changes fastest.
Arguments:
- left_feat: bfloat16 [4, 256, 320], P(('tiles', 'rows'), ('cols', 'disp')), parts along dimension 0, may hold values from -64 to 64
- right_feat: bfloat16 [4, 256, 320], P(('tiles', 'rows'), ('cols', 'disp')), parts along dimension 0, may hold values from -64 to 64
- conv_first: bfloat16 [27, 32, 40], replicated, may hold values from -0.1875 to 0.1875
- conv_mid: bfloat16 [2, 27, 32, 32], replicated, may hold values from -0.21875 to 0.21875
- conv_last: bfloat16 [27, 1, 32], replicated, may hold values from -3 to 3
Outputs:
- estimate: float32 [4, 256], P(('tiles', 'rows'), ('cols', 'disp')), parts along dimension 0
The draws below stay inside these ranges and needn't reach their ends.
There are 2 independent parts, one for each index of `tiles`. The reference program is written for one: setup_inputs(seed, part) draws one part's arguments, and reference() takes and returns one part's arrays. A program takes and returns all parts, laid end to end along the dimension named above; an argument that names none is the same for every part. Nothing has to cross between parts.
All inputs are finite; a program needn't handle non-finite values.
Results may differ from the reference program's by a relative error of at most 0.012.
The reference program's roundings to bfloat16 on the way (of `volume`) count: a program that leaves them out, or rounds other values in their place, can miss the bound.
Values may be sent and summed in bfloat16 or wider, within the bound.
A program may use at most 64 MiB of HBM per device.

```python
import jax
import jax.numpy as jnp
from jax import lax

C = 320
G = 40
F = 32
MID = 2
DISP = 64
H = 2
W = 256


def boost_rows(key):
    base = jax.random.fold_in(key, 7)
    pick_key, mask_key, level_key = jax.random.split(base, 3)
    pick = jax.random.randint(pick_key, (), 0, H)
    chosen = (jax.random.randint(mask_key, (H,), 0, 8) == 0) | (jnp.arange(H) == pick)
    levels = jnp.array([7.0, 9.0, 11.0], jnp.float32)[jax.random.randint(level_key, (H,), 0, 3)]
    return jnp.where(chosen, levels, 1.0).astype(jnp.float32)[:, None, None]


def draw_features(key, salt):
    boost = boost_rows(key)
    own_key = jax.random.fold_in(key, salt)
    first_key = jax.random.fold_in(own_key, 0)
    values = jnp.clip(jax.random.normal(first_key, (H, W, C), jnp.float32), -4.0, 4.0)
    values = values * boost
    return values.astype(jnp.bfloat16)


def draw_left_feat(key, part):
    return draw_features(key, 11)


def draw_right_feat(key, part):
    return draw_features(key, 12)


def noise(key, extent, deviation, limit, held_as=jnp.bfloat16):
    result = deviation * jax.random.normal(key, extent, jnp.float32)
    return jnp.clip(result, min=-limit, max=limit).astype(held_as)


def setup_inputs(seed: int = 0, part: int = 0) -> dict:
    streams_of = jax.random.split(jax.random.key(seed), 6)
    part_splits = jax.random.split(jax.random.fold_in(streams_of[5], part), 6)
    return {
        "left_feat": draw_left_feat(jax.random.fold_in(jax.random.fold_in(streams_of[5], part), 71), part),
        "right_feat": draw_right_feat(jax.random.fold_in(jax.random.fold_in(streams_of[5], part), 71), part),
        "conv_first": noise(streams_of[2], (27, F, G), (27 * G) ** -0.5, 0.1875),
        "conv_mid": noise(streams_of[3], (MID, 27, F, F), (27 * F) ** -0.5, 0.21875),
        "conv_last": noise(streams_of[4], (27, 1, F), 0.5, 3.0),
    }


def conv_layer(inputs, kernel):
    taps = jnp.transpose(kernel, (1, 2, 0)).reshape(kernel.shape[1], kernel.shape[2], 3, 3, 3).astype(jnp.float32)
    planes = jnp.transpose(inputs, (1, 0, 2, 3))[None].astype(jnp.float32)
    output = lax.conv_general_dilated(planes, taps, (1, 1, 1), ((1, 1), (1, 1), (1, 1)), dimension_numbers=("NCDHW", "OIDHW", "NCDHW"), precision=lax.Precision.HIGHEST)
    return jnp.transpose(output[0], (1, 0, 2, 3))


def reference(left_feat, right_feat, conv_first, conv_mid, conv_last):
    group_size = C // G
    padded_right = jnp.pad(right_feat, ((0, 0), (DISP, 0), (0, 0)))
    left_groups = left_feat.astype(jnp.float32).reshape(H, W, G, group_size)

    def single(disp_value):
        shifted = lax.dynamic_slice_in_dim(padded_right, (DISP - disp_value).astype(jnp.int32), W, 1)
        right_groups = shifted.astype(jnp.float32).reshape(H, W, G, group_size)
        corr = jnp.sum(left_groups * right_groups, axis=3) / group_size
        return jnp.transpose(corr, (2, 0, 1)).astype(jnp.bfloat16)

    volume = lax.map(single, jnp.arange(DISP, dtype=jnp.int32))
    hidden = jax.nn.relu(conv_layer(volume, conv_first))
    for layer in range(MID):
        hidden = jax.nn.relu(conv_layer(hidden, conv_mid[layer]))
    cost_cube = conv_layer(hidden, conv_last)[:, 0]
    highest = jnp.max(cost_cube, axis=0)
    weights = jnp.exp(cost_cube - highest[None])
    levels = (jnp.arange(DISP, dtype=jnp.float32) / DISP)[:, None, None]
    return jnp.sum(weights * levels, axis=0) / jnp.sum(weights, axis=0)
```

```python
import functools

import jax
import jax.numpy as jnp
import numpy as np
from jax import lax
from jax.experimental import pallas as pl
from jax.experimental.pallas import tpu as pltpu
from jax.sharding import PartitionSpec as P

MID = 2
DDEV = 16


def extended_2(block, sides, width):
    for axis, dim in sides:
        count = lax.axis_size(axis)
        forward = [(i, i + 1) for i in range(count - 1)]
        backward = [(target, source) for source, target in forward]
        low = lax.ppermute(
            lax.slice_in_dim(block, block.shape[dim] - width, None, axis=dim), axis, forward
        )
        high = lax.ppermute(lax.slice_in_dim(block, 0, width, axis=dim), axis, backward)
        block = jnp.concatenate([low, block, high], axis=dim)
    return block


def passed_along(x, axis, by):
    peers = lax.axis_size(axis)
    pairs = [(i, i + by) for i in range(peers) if 0 <= i + by < peers]
    return lax.ppermute(x, axis, pairs)


def combined_all(part, axis, combine):
    gathered = jax.tree.map(lambda a: lax.all_gather(a, axis), part)

    def take(source):
        return jax.tree.map(lambda a: lax.dynamic_index_in_dim(a, source, 0, False), gathered)

    return lax.fori_loop(
        1, lax.axis_size(axis), lambda source, state: combine(state, take(source)), take(0)
    )


def correlate(left_full, extended, groups, first_disp, count, total_disp):
    rows_here, width_here, channels = left_full.shape
    group_size = channels // groups
    left_groups = left_full.reshape(rows_here, width_here, groups, group_size)

    def single(offset):
        disp_value = first_disp + offset
        shifted = lax.dynamic_slice_in_dim(extended, 2 * width_here - disp_value, width_here, 1)
        right_groups = shifted.reshape(rows_here, width_here, groups, group_size)
        corr = (
            jnp.einsum(
                "hwgc,hwgc->ghw", left_groups, right_groups, preferred_element_type=jnp.float32
            )
            / group_size
        )
        inside = (disp_value >= 0) & (disp_value < total_disp)
        return jnp.where(inside, corr, 0.0).astype(jnp.bfloat16)

    return lax.map(single, jnp.arange(count, dtype=jnp.int32))


def convolve(padded, kernel):
    depth_out = padded.shape[0] - 2
    in_chans = padded.shape[1]
    rows_out = padded.shape[2] - 2
    cols_out = padded.shape[3] - 2
    out_chans = kernel.shape[1]
    columns = jnp.concatenate(
        [
            padded[:, :, row_tap : row_tap + rows_out, col_tap : col_tap + cols_out]
            for row_tap in range(3)
            for col_tap in range(3)
        ],
        axis=1,
    )
    flat = columns.reshape(depth_out + 2, 9 * in_chans, rows_out * cols_out)
    summed = jnp.zeros((depth_out, out_chans, rows_out * cols_out), jnp.float32)
    for disp_tap in range(3):
        taps = (
            jnp.transpose(kernel[9 * disp_tap : 9 * disp_tap + 9], (1, 0, 2))
            .reshape(out_chans, 9 * in_chans)
            .astype(flat.dtype)
        )
        summed = summed + jnp.einsum(
            "ok,dkn->don",
            taps,
            flat[disp_tap : disp_tap + depth_out],
            preferred_element_type=jnp.float32,
            precision=lax.Precision.HIGHEST,
        )
    return summed.reshape(depth_out, out_chans, rows_out, cols_out)


def widen(hidden):
    return extended_2(hidden, (("disp", 0), ("rows", 2), ("cols", 3)), 1)


def combine_parts(earlier, later):
    highest = jnp.maximum(earlier[0], later[0])
    scale_one = jnp.exp(earlier[0] - highest)
    scale_two = jnp.exp(later[0] - highest)
    return (
        highest,
        earlier[1] * scale_one + later[1] * scale_two,
        earlier[2] * scale_one + later[2] * scale_two,
    )


def shards(left_feat, right_feat, conv_first, conv_mid, conv_last):
    piece_width = left_feat.shape[1]
    groups = conv_first.shape[2]
    disp_count = lax.axis_size("disp")
    depth_here = DDEV
    total_disp = depth_here * disp_count
    first_disp = lax.axis_index("disp") * depth_here
    left_full, right_full = (
        lax.all_gather(left_feat, "disp", axis=1, tiled=True),
        lax.all_gather(right_feat, "disp", axis=1, tiled=True),
    )
    prior_full = passed_along(right_full, "cols", 1)
    extended = jnp.concatenate([jnp.zeros_like(right_full), prior_full, right_full], axis=1)
    volume = correlate(left_full, extended, groups, first_disp, depth_here, total_disp)
    padded = extended_2(volume, (("disp", 0), ("rows", 2), ("cols", 3)), 1)
    hidden = jax.nn.relu(convolve(padded, conv_first))
    for layer in range(MID):
        hidden = jax.nn.relu(convolve(widen(hidden), conv_mid[layer]))
    cost_cube = convolve(widen(hidden), conv_last)[:, 0]
    levels = (
        (first_disp + jnp.arange(depth_here, dtype=jnp.int32)).astype(jnp.float32) / total_disp
    )[:, None, None]
    local_high = jnp.max(cost_cube, axis=0)
    weights = jnp.exp(cost_cube - local_high[None])
    merged = combined_all(
        (local_high, jnp.sum(weights, axis=0), jnp.sum(weights * levels, axis=0)),
        "disp",
        combine_parts,
    )
    whole_row = merged[2] / merged[1]
    return lax.dynamic_slice_in_dim(whole_row, lax.axis_index("disp") * piece_width, piece_width, 1)


HALO = 4
GROUP = 4


def permutation(channels, groups):
    size = channels // groups
    out = np.zeros((2 * channels, size * 128), np.float32)
    for row in range(2):
        for c in range(channels):
            out[row * channels + c, (c % size) * 128 + row * 64 + c // size] = 1
    return out


def tap_choice():
    out = np.zeros((GROUP + 2, 2, GROUP, 2, 3, 3), np.float32)
    for d_in in range(GROUP + 2):
        for d_out in range(GROUP):
            for r_in in range(2):
                for r_out in range(2):
                    if 0 <= d_in - d_out <= 2:
                        out[d_in, r_in, d_out, r_out, d_in - d_out, r_in - r_out + 1] = 1
    return out


def banded(kernel):
    outs, ins = kernel.shape[1:]
    taps = kernel.reshape(3, 3, 3, outs, ins)
    choice = jnp.asarray(tap_choice(), jnp.bfloat16)
    return jnp.einsum(
        "drqsab,abeoi->drieqso", choice, taps, preferred_element_type=jnp.bfloat16
    )


def whole_kernel(
    disps, width_all, feat_ref, perm_ref, first_ref, mid_ref, last_ref, out_ref, a_ref, p_ref, f_ref
):
    width_here = out_ref.shape[1]
    wide = width_here + 2 * HALO
    span = disps + wide
    groups_d = disps // GROUP + 1
    rows = groups_d * wide
    f_ref[...] = jnp.dot(feat_ref[...], perm_ref[...], preferred_element_type=jnp.float32)
    a_ref[...] = jnp.zeros_like(a_ref)
    size = f_ref.shape[1] // 128
    for d in range(disps):
        acc = None
        for k in range(size):
            lanes = slice(128 * k, 128 * k + 128)
            start = wide + disps - d
            term = f_ref[0:wide, lanes] * f_ref[start : start + wide, lanes]
            acc = term if acc is None else acc + term
        slab = (acc / size).astype(jnp.bfloat16)
        stored = d + HALO
        group, place = divmod(stored, GROUP)
        a_ref[group * wide : (group + 1) * wide, 128 * place : 128 * place + 128] = slab
        if place < 2 and group > 0:
            lane = 128 * (GROUP + place)
            a_ref[(group - 1) * wide : group * wide, lane : lane + 128] = slab

    piece = lax.axis_index("cols") * lax.axis_size("disp") + lax.axis_index("disp")
    column = piece * width_here - HALO + lax.broadcasted_iota(jnp.int32, (wide, 256), 0)
    in_image = (column >= 0) & (column < width_all)
    lane_disp = lax.broadcasted_iota(jnp.int32, (wide, 256), 1) // 64

    for layer in range(MID + 1):
        taps_ref = first_ref if layer == 0 else mid_ref.at[layer - 1]
        if layer == 0:
            p_ref[8 : 8 + rows, :] = jnp.dot(
                a_ref[...], taps_ref[...], preferred_element_type=jnp.float32
            )
        else:
            taps = taps_ref[...]
            p_ref[8 : 8 + rows, :] = jnp.dot(
                a_ref[...],
                jnp.concatenate([taps, taps], axis=0),
                preferred_element_type=jnp.float32,
            )
        base = layer + 1 - HALO
        for group in range(groups_d):
            at = 8 + group * wide
            total = (
                p_ref[at - 1 : at - 1 + wide, 0:256]
                + p_ref[at : at + wide, 256:512]
                + p_ref[at + 1 : at + 1 + wide, 512:768]
            )
            low = base + GROUP * group
            keep = in_image
            if low < 0 or low + GROUP > disps:
                keep = keep & (lane_disp >= -low) & (lane_disp < disps - low)
            total = jnp.where(keep, jnp.maximum(total, 0.0), 0.0)
            high = total.astype(jnp.bfloat16)
            rest = (total - high.astype(jnp.float32)).astype(jnp.bfloat16)
            here = slice(group * wide, (group + 1) * wide)
            a_ref[here, 0:256] = high
            a_ref[here, 384:640] = rest
            if group > 0:
                before = slice((group - 1) * wide, group * wide)
                a_ref[before, 256:384] = high[:, 0:128]
                a_ref[before, 640:768] = rest[:, 0:128]
            if group == groups_d - 1:
                a_ref[here, 256:384] = jnp.zeros((wide, 128), jnp.bfloat16)
                a_ref[here, 640:768] = jnp.zeros((wide, 128), jnp.bfloat16)

    used = (groups_d - 1) * wide
    taps = last_ref[...]
    p_ref[8 : 8 + used, 0:384] = jnp.dot(
        a_ref[0:used], jnp.concatenate([taps, taps], axis=0), preferred_element_type=jnp.float32
    )
    costs = []
    for group in range(groups_d - 1):
        at = 8 + group * wide
        costs.append(
            p_ref[at - 1 : at - 1 + wide, 0:128]
            + p_ref[at : at + wide, 128:256]
            + p_ref[at + 1 : at + 1 + wide, 256:384]
        )
    lane = lax.broadcasted_iota(jnp.int32, (wide, 128), 1)
    mine = lane % 2 == lax.axis_index("rows")
    mine = mine & (lane < 2 * GROUP)
    top = functools.reduce(jnp.maximum, costs)
    top = jnp.max(jnp.where(mine, top, -jnp.inf), axis=1, keepdims=True)
    weight_sum = jnp.zeros((wide, 128), jnp.float32)
    level_sum = jnp.zeros((wide, 128), jnp.float32)
    for group, cost in enumerate(costs):
        weight = jnp.where(mine, jnp.exp(jnp.where(mine, cost - top, 0.0)), 0.0)
        level = (lane // 2 + GROUP * group).astype(jnp.float32) * (1.0 / disps)
        weight_sum += weight
        level_sum += weight * level
    estimate = jnp.sum(level_sum, axis=1, keepdims=True) / jnp.sum(
        weight_sum, axis=1, keepdims=True
    )
    place = lax.broadcasted_iota(jnp.int32, (wide, 128), 0)
    line = jnp.sum(jnp.where(place == lane + HALO, estimate, 0.0), axis=0, keepdims=True)
    out_ref[...] = line[:, 0:width_here]


def gathered_features(left_feat, right_feat, disps):
    width = left_feat.shape[1]
    both = jnp.concatenate([left_feat, right_feat], axis=0)
    other = lax.ppermute(both, "rows", [(0, 1), (1, 0)])
    first = lax.axis_index("rows") == 0
    pair = jnp.concatenate([jnp.where(first, both, other), jnp.where(first, other, both)], axis=2)
    peers = lax.axis_size("cols") * lax.axis_size("disp")

    def at(piece):
        col, disp = divmod(piece, lax.axis_size("disp"))
        return disp * lax.axis_size("cols") + col

    def moved(x, by):
        pairs = [(at(i), at(i + by)) for i in range(peers) if 0 <= i + by < peers]
        return lax.ppermute(x, ("disp", "cols"), pairs)

    left, right = pair[0], pair[1]
    after = moved(pair[:, :HALO], -1)
    before_left = moved(left[width - HALO :], 1)
    before = []
    needed = disps + HALO
    by = 1
    while needed > 0:
        take = min(width, needed)
        before.insert(0, moved(right[width - take :], by))
        needed -= take
        by += 1
    return jnp.concatenate(
        [before_left, left, after[0]] + before + [right, after[1]], axis=0
    )


def window_shards(left_feat, right_feat, conv_first, conv_mid, conv_last):
    width = left_feat.shape[1]
    channels = left_feat.shape[2]
    groups = conv_first.shape[2]
    disps = DDEV * lax.axis_size("disp")
    width_all = width * lax.axis_size("disp") * lax.axis_size("cols")
    feats = gathered_features(left_feat, right_feat, disps)
    perm = jnp.asarray(permutation(channels, groups), jnp.bfloat16)
    first = banded(jnp.pad(conv_first, ((0, 0), (0, 0), (0, 64 - groups)))).reshape(768, 768)
    mid = jax.vmap(banded)(conv_mid).reshape(MID, 384, 768)
    last = banded(conv_last).reshape(384, 3, 8)
    last = jnp.pad(last, ((0, 0), (0, 0), (0, 120))).reshape(384, 384)
    wide = width + 2 * HALO
    rows = (disps // GROUP + 1) * wide
    return pl.pallas_call(
        functools.partial(whole_kernel, disps, width_all),
        out_shape=jax.ShapeDtypeStruct((1, width), jnp.float32),
        in_specs=[pl.BlockSpec(memory_space=pltpu.VMEM)] * 5,
        out_specs=pl.BlockSpec(memory_space=pltpu.VMEM),
        scratch_shapes=[
            pltpu.VMEM((rows, 768), jnp.bfloat16),
            pltpu.VMEM((rows + 16, 768), jnp.float32),
            pltpu.VMEM((2 * wide + disps, (channels // groups) * 128), jnp.float32),
        ],
        compiler_params=pltpu.CompilerParams(vmem_limit_bytes=48 * 1024 * 1024),
    )(feats, perm, first, mid, last)


def solution(mesh):
    rows, pieces = mesh.shape["rows"], mesh.shape["cols"] * mesh.shape["disp"]
    body = window_shards if rows == 2 and pieces == 8 else shards
    return jax.shard_map(
        body,
        mesh=mesh,
        in_specs=(
            P(("tiles", "rows"), ("cols", "disp"), None),
            P(("tiles", "rows"), ("cols", "disp"), None),
            P(),
            P(),
            P(),
        ),
        out_specs=P(("tiles", "rows"), ("cols", "disp")),
        check_vma=False,
    )
```

```python
import functools

import jax
import jax.numpy as jnp
from jax import lax
from jax.experimental import pallas as pl
from jax.experimental.pallas import tpu as pltpu
from jax.sharding import PartitionSpec as P

MID = 2
DDEV = 16


def extended_2(block, sides, width):
    for axis, dim in sides:
        count = lax.axis_size(axis)
        forward = [(i, i + 1) for i in range(count - 1)]
        backward = [(target, source) for source, target in forward]
        low = lax.ppermute(
            lax.slice_in_dim(block, block.shape[dim] - width, None, axis=dim), axis, forward
        )
        high = lax.ppermute(lax.slice_in_dim(block, 0, width, axis=dim), axis, backward)
        block = jnp.concatenate([low, block, high], axis=dim)
    return block


def passed_along(x, axis, by):
    peers = lax.axis_size(axis)
    pairs = [(i, i + by) for i in range(peers) if 0 <= i + by < peers]
    return lax.ppermute(x, axis, pairs)


def combined_all(part, axis, combine):
    gathered = jax.tree.map(lambda a: lax.all_gather(a, axis), part)

    def take(source):
        return jax.tree.map(lambda a: lax.dynamic_index_in_dim(a, source, 0, False), gathered)

    return lax.fori_loop(
        1, lax.axis_size(axis), lambda source, state: combine(state, take(source)), take(0)
    )


def correlate(left_full, extended, groups, first_disp, count, total_disp):
    rows_here, width_here, channels = left_full.shape
    group_size = channels // groups
    left_groups = left_full.reshape(rows_here, width_here, groups, group_size)

    def single(offset):
        disp_value = first_disp + offset
        shifted = lax.dynamic_slice_in_dim(extended, 2 * width_here - disp_value, width_here, 1)
        right_groups = shifted.reshape(rows_here, width_here, groups, group_size)
        corr = (
            jnp.einsum(
                "hwgc,hwgc->ghw", left_groups, right_groups, preferred_element_type=jnp.float32
            )
            / group_size
        )
        inside = (disp_value >= 0) & (disp_value < total_disp)
        return jnp.where(inside, corr, 0.0).astype(jnp.bfloat16)

    return lax.map(single, jnp.arange(count, dtype=jnp.int32))


def convolve(padded, kernel):
    depth_out = padded.shape[0] - 2
    in_chans = padded.shape[1]
    rows_out = padded.shape[2] - 2
    cols_out = padded.shape[3] - 2
    out_chans = kernel.shape[1]
    columns = jnp.concatenate(
        [
            padded[:, :, row_tap : row_tap + rows_out, col_tap : col_tap + cols_out]
            for row_tap in range(3)
            for col_tap in range(3)
        ],
        axis=1,
    )
    flat = columns.reshape(depth_out + 2, 9 * in_chans, rows_out * cols_out)
    summed = jnp.zeros((depth_out, out_chans, rows_out * cols_out), jnp.float32)
    for disp_tap in range(3):
        taps = (
            jnp.transpose(kernel[9 * disp_tap : 9 * disp_tap + 9], (1, 0, 2))
            .reshape(out_chans, 9 * in_chans)
            .astype(flat.dtype)
        )
        summed = summed + jnp.einsum(
            "ok,dkn->don",
            taps,
            flat[disp_tap : disp_tap + depth_out],
            preferred_element_type=jnp.float32,
            precision=lax.Precision.HIGHEST,
        )
    return summed.reshape(depth_out, out_chans, rows_out, cols_out)


def widen(hidden):
    return extended_2(hidden, (("disp", 0), ("rows", 2), ("cols", 3)), 1)


def combine_parts(earlier, later):
    highest = jnp.maximum(earlier[0], later[0])
    scale_one = jnp.exp(earlier[0] - highest)
    scale_two = jnp.exp(later[0] - highest)
    return (
        highest,
        earlier[1] * scale_one + later[1] * scale_two,
        earlier[2] * scale_one + later[2] * scale_two,
    )


def shards(left_feat, right_feat, conv_first, conv_mid, conv_last):
    piece_width = left_feat.shape[1]
    groups = conv_first.shape[2]
    disp_count = lax.axis_size("disp")
    depth_here = DDEV
    total_disp = depth_here * disp_count
    first_disp = lax.axis_index("disp") * depth_here
    left_full, right_full = (
        lax.all_gather(left_feat, "disp", axis=1, tiled=True),
        lax.all_gather(right_feat, "disp", axis=1, tiled=True),
    )
    prior_full = passed_along(right_full, "cols", 1)
    extended = jnp.concatenate([jnp.zeros_like(right_full), prior_full, right_full], axis=1)
    volume = correlate(left_full, extended, groups, first_disp, depth_here, total_disp)
    padded = extended_2(volume, (("disp", 0), ("rows", 2), ("cols", 3)), 1)
    hidden = jax.nn.relu(convolve(padded, conv_first))
    for layer in range(MID):
        hidden = jax.nn.relu(convolve(widen(hidden), conv_mid[layer]))
    cost_cube = convolve(widen(hidden), conv_last)[:, 0]
    levels = (
        (first_disp + jnp.arange(depth_here, dtype=jnp.int32)).astype(jnp.float32) / total_disp
    )[:, None, None]
    local_high = jnp.max(cost_cube, axis=0)
    weights = jnp.exp(cost_cube - local_high[None])
    merged = combined_all(
        (local_high, jnp.sum(weights, axis=0), jnp.sum(weights * levels, axis=0)),
        "disp",
        combine_parts,
    )
    whole_row = merged[2] / merged[1]
    return lax.dynamic_slice_in_dim(whole_row, lax.axis_index("disp") * piece_width, piece_width, 1)


HALO = 4
GROUP = 4


EDGE = 16


def permutation(row, channels, groups):
    size = channels // groups
    lane = lax.broadcasted_iota(jnp.int32, (1, 128 * size), 1)
    group = lane % 64
    wanted = group * size + lane // 128
    wanted = jnp.where((group < groups) & ((lane // 64) % 2 == row), wanted, -1)
    channel = lax.broadcasted_iota(jnp.int32, (channels, 128 * size), 0)
    return (channel == wanted).astype(jnp.float32).astype(jnp.bfloat16)


def tap_of(a, r_in, r_out, e):
    return 9 * a + 3 * (r_in - r_out + 1) + e


def build_first(taps_ref, banded_ref):
    banded_ref[...] = jnp.zeros_like(banded_ref)
    outs, ins = taps_ref.shape[1:]
    blank = jnp.zeros((outs, 64 - ins), jnp.float32)
    for e in range(3):
        for r_out in range(2):
            for a in range(3):
                slabs = []
                for r_in in range(2):
                    slabs += [taps_ref[tap_of(a, r_in, r_out, e)].astype(jnp.float32), blank]
                block = jnp.concatenate(slabs, axis=1).astype(jnp.bfloat16)
                for d_out in range(GROUP):
                    at = e * 256 + d_out * 64 + r_out * 32
                    lane = 128 * (d_out + a)
                    banded_ref[at : at + outs, lane : lane + 128] = block


def build_mid(taps_ref, banded_ref):
    banded_ref[...] = jnp.zeros_like(banded_ref)
    outs = taps_ref.shape[1]
    blank = jnp.zeros((outs, 64), jnp.float32)
    for e in range(3):
        for r_out in range(2):
            slabs = [
                taps_ref[tap_of(a, r_in, r_out, e)].astype(jnp.float32)
                for a in range(3)
                for r_in in range(2)
            ]
            even = jnp.concatenate(slabs + [blank], axis=1).astype(jnp.bfloat16)
            odd = jnp.concatenate([blank] + slabs, axis=1).astype(jnp.bfloat16)
            for d_out in range(GROUP):
                at = e * 256 + d_out * 64 + r_out * 32
                block = even if d_out % 2 == 0 else odd
                for lane in (128 * (d_out // 2), 384 + 128 * (d_out // 2)):
                    banded_ref[at : at + outs, lane : lane + 256] = block


def build_last(taps_ref, banded_ref):
    banded_ref[...] = jnp.zeros_like(banded_ref)
    for e in range(3):
        lines = []
        for d_out in range(GROUP):
            for r_out in range(2):
                parts = [
                    taps_ref[tap_of(a, r_in, r_out, e)].astype(jnp.float32)
                    for a in range(3)
                    for r_in in range(2)
                ]
                if d_out > 0:
                    parts.insert(0, jnp.zeros((1, 64 * d_out), jnp.float32))
                if d_out < GROUP - 1:
                    parts.append(jnp.zeros((1, 64 * (GROUP - 1 - d_out)), jnp.float32))
                lines.append(jnp.concatenate(parts, axis=1))
        lines.append(jnp.zeros((8, 384), jnp.float32))
        block = jnp.concatenate(lines, axis=0).astype(jnp.bfloat16)
        banded_ref[128 * e : 128 * e + 16, 0:384] = block
        banded_ref[128 * e : 128 * e + 16, 384:768] = block


def across(x, banded):
    return lax.dot_general(
        x, banded, (((1,), (1,)), ((), ())), preferred_element_type=jnp.float32
    )


def whole_kernel(
    disps,
    width_all,
    feat_ref,
    first_taps,
    mid_taps,
    last_taps,
    out_ref,
    a_ref,
    p_ref,
    f_ref,
    first_ref,
    mid_ref,
    last_ref,
):
    width_here = out_ref.shape[1]
    wide = width_here + 2 * HALO
    span = disps + wide
    groups_d = disps // GROUP + 1
    rows = groups_d * wide
    build_first(first_taps, first_ref)
    for layer in range(MID):
        build_mid(mid_taps.at[layer], mid_ref.at[layer])
    build_last(last_taps, last_ref)
    channels, groups = feat_ref.shape[2], first_taps.shape[2]
    f_ref[...] = jnp.dot(
        feat_ref[0], permutation(0, channels, groups), preferred_element_type=jnp.float32
    ) + jnp.dot(
        feat_ref[1], permutation(1, channels, groups), preferred_element_type=jnp.float32
    )
    left_at = EDGE - HALO
    right_at = width_here + 2 * EDGE + EDGE - HALO
    a_ref[...] = jnp.zeros_like(a_ref)
    size = f_ref.shape[1] // 128
    for d in range(disps):
        acc = None
        for k in range(size):
            lanes = slice(128 * k, 128 * k + 128)
            start = right_at + disps - d
            term = f_ref[left_at : left_at + wide, lanes] * f_ref[start : start + wide, lanes]
            acc = term if acc is None else acc + term
        slab = (acc / size).astype(jnp.bfloat16)
        stored = d + HALO
        group, place = divmod(stored, GROUP)
        a_ref[group * wide : (group + 1) * wide, 128 * place : 128 * place + 128] = slab
        if place < 2 and group > 0:
            lane = 128 * (GROUP + place)
            a_ref[(group - 1) * wide : group * wide, lane : lane + 128] = slab

    piece = lax.axis_index("cols") * lax.axis_size("disp") + lax.axis_index("disp")
    column = piece * width_here - HALO + lax.broadcasted_iota(jnp.int32, (wide, 256), 0)
    in_image = (column >= 0) & (column < width_all)
    lane_disp = lax.broadcasted_iota(jnp.int32, (wide, 256), 1) // 64

    for layer in range(MID + 1):
        taps_ref = first_ref if layer == 0 else mid_ref.at[layer - 1]
        p_ref[8 : 8 + rows, :] = across(a_ref[...], taps_ref[...])
        base = layer + 1 - HALO
        for group in range(groups_d):
            at = 8 + group * wide
            total = (
                p_ref[at - 1 : at - 1 + wide, 0:256]
                + p_ref[at : at + wide, 256:512]
                + p_ref[at + 1 : at + 1 + wide, 512:768]
            )
            low = base + GROUP * group
            keep = in_image
            if low < 0 or low + GROUP > disps:
                keep = keep & (lane_disp >= -low) & (lane_disp < disps - low)
            total = jnp.where(keep, jnp.maximum(total, 0.0), 0.0)
            high = total.astype(jnp.bfloat16)
            rest = (total - high.astype(jnp.float32)).astype(jnp.bfloat16)
            here = slice(group * wide, (group + 1) * wide)
            a_ref[here, 0:256] = high
            a_ref[here, 384:640] = rest
            if group > 0:
                before = slice((group - 1) * wide, group * wide)
                a_ref[before, 256:384] = high[:, 0:128]
                a_ref[before, 640:768] = rest[:, 0:128]
            if group == groups_d - 1:
                a_ref[here, 256:384] = jnp.zeros((wide, 128), jnp.bfloat16)
                a_ref[here, 640:768] = jnp.zeros((wide, 128), jnp.bfloat16)

    used = (groups_d - 1) * wide
    p_ref[8 : 8 + used, 0:384] = across(a_ref[0:used], last_ref[...])
    costs = []
    for group in range(groups_d - 1):
        at = 8 + group * wide
        costs.append(
            p_ref[at - 1 : at - 1 + wide, 0:128]
            + p_ref[at : at + wide, 128:256]
            + p_ref[at + 1 : at + 1 + wide, 256:384]
        )
    lane = lax.broadcasted_iota(jnp.int32, (wide, 128), 1)
    mine = lane % 2 == lax.axis_index("rows")
    mine = mine & (lane < 2 * GROUP)
    top = functools.reduce(jnp.maximum, costs)
    top = jnp.max(jnp.where(mine, top, -jnp.inf), axis=1, keepdims=True)
    weight_sum = jnp.zeros((wide, 128), jnp.float32)
    level_sum = jnp.zeros((wide, 128), jnp.float32)
    for group, cost in enumerate(costs):
        weight = jnp.where(mine, jnp.exp(jnp.where(mine, cost - top, 0.0)), 0.0)
        level = (lane // 2 + GROUP * group).astype(jnp.float32) * (1.0 / disps)
        weight_sum += weight
        level_sum += weight * level
    estimate = jnp.sum(level_sum, axis=1, keepdims=True) / jnp.sum(
        weight_sum, axis=1, keepdims=True
    )
    place = lax.broadcasted_iota(jnp.int32, (wide, 128), 0)
    line = jnp.sum(jnp.where(place == lane + HALO, estimate, 0.0), axis=0, keepdims=True)
    out_ref[...] = line[:, 0:width_here]


def exchange_kernel(copies, left_ref, right_ref, out_ref, held, send_sem, recv_sem):
    width = left_ref.shape[1]
    row, col, disp = lax.axis_index("rows"), lax.axis_index("cols"), lax.axis_index("disp")
    col_disps = lax.axis_size("disp")
    pieces = col_disps * lax.axis_size("cols")
    piece = col * col_disps + disp
    held[...] = jnp.zeros_like(held)

    def device(other, by):
        target = piece + by
        return {
            "tiles": lax.axis_index("tiles"),
            "disp": target % col_disps,
            "rows": (row + other) % 2,
            "cols": target // col_disps,
        }

    def exists(by):
        return (piece + by >= 0) & (piece + by < pieces)

    barrier = pltpu.get_barrier_semaphore()
    partners = jnp.int32(0)
    for by in range(-3, 4):
        for other in range(2):
            if by == 0 and other == 0:
                continue

            @pl.when(exists(by))
            def _():
                pl.semaphore_signal(
                    barrier,
                    inc=1,
                    device_id=device(other, by),
                    device_id_type=pl.DeviceIdType.MESH,
                )

            partners = partners + exists(by).astype(jnp.int32)
    pl.semaphore_wait(barrier, partners)

    def copy(number):
        view, by, other, source, target, count = copies[number]
        return pltpu.make_async_remote_copy(
            src_ref=(left_ref if view == 0 else right_ref).at[0, pl.ds(source, count)],
            dst_ref=held.at[row, pl.ds(target, count)],
            send_sem=send_sem.at[number],
            recv_sem=recv_sem.at[number],
            device_id=device(other, by),
            device_id_type=pl.DeviceIdType.MESH,
        )

    for number in range(len(copies)):

        @pl.when(exists(copies[number][1]))
        def _():
            copy(number).start()

    held[row, EDGE : EDGE + width] = left_ref[0]
    own = width + 3 * EDGE + 2 * width
    held[row, own : own + width] = right_ref[0]
    for number in range(len(copies)):
        by = copies[number][1]

        @pl.when(exists(by))
        def _():
            copy(number).wait_send()

        @pl.when(exists(-by))
        def _():
            copy(number).wait_recv()

    out_ref[...] = held[...]


def exchanged(left_feat, right_feat):
    width, channels = left_feat.shape[1:]
    right_at = width + 2 * EDGE
    own = right_at + EDGE + 2 * width
    copies = []
    for other in (1, 0):
        copies.append((1, 2, other, 0, own - 2 * width, width))
        copies.append((1, 3, other, width - EDGE, right_at, EDGE))
        copies.append((1, 1, other, 0, own - width, width))
        copies.append((1, -1, other, 0, own + width, EDGE))
        copies.append((0, 1, other, width - EDGE, 0, EDGE))
        copies.append((0, -1, other, 0, EDGE + width, EDGE))
    copies.append((1, 0, 1, 0, own, width))
    copies.append((0, 0, 1, 0, EDGE, width))
    shape = (2, own + width + EDGE, channels)
    return pl.pallas_call(
        functools.partial(exchange_kernel, tuple(copies)),
        out_shape=jax.ShapeDtypeStruct(shape, jnp.bfloat16),
        in_specs=[pl.BlockSpec(memory_space=pltpu.VMEM)] * 2,
        out_specs=pl.BlockSpec(memory_space=pltpu.VMEM),
        scratch_shapes=[
            pltpu.VMEM(shape, jnp.bfloat16),
            pltpu.SemaphoreType.DMA((len(copies),)),
            pltpu.SemaphoreType.DMA((len(copies),)),
        ],
        compiler_params=pltpu.CompilerParams(collective_id=0, has_side_effects=True),
    )(left_feat, right_feat)


def window_shards(left_feat, right_feat, conv_first, conv_mid, conv_last):
    width = left_feat.shape[1]
    channels = left_feat.shape[2]
    groups = conv_first.shape[2]
    disps = DDEV * lax.axis_size("disp")
    width_all = width * lax.axis_size("disp") * lax.axis_size("cols")
    feats = exchanged(left_feat, right_feat)
    wide = width + 2 * HALO
    rows = (disps // GROUP + 1) * wide
    return pl.pallas_call(
        functools.partial(whole_kernel, disps, width_all),
        out_shape=jax.ShapeDtypeStruct((1, width), jnp.float32),
        in_specs=[pl.BlockSpec(memory_space=pltpu.VMEM)] * 4,
        out_specs=pl.BlockSpec(memory_space=pltpu.VMEM),
        scratch_shapes=[
            pltpu.VMEM((rows, 768), jnp.bfloat16),
            pltpu.VMEM((rows + 16, 768), jnp.float32),
            pltpu.VMEM((feats.shape[1], (channels // groups) * 128), jnp.float32),
            pltpu.VMEM((768, 768), jnp.bfloat16),
            pltpu.VMEM((MID, 768, 768), jnp.bfloat16),
            pltpu.VMEM((384, 768), jnp.bfloat16),
        ],
        compiler_params=pltpu.CompilerParams(vmem_limit_bytes=48 * 1024 * 1024),
    )(feats, conv_first, conv_mid, conv_last)


def solution(mesh):
    rows, pieces = mesh.shape["rows"], mesh.shape["cols"] * mesh.shape["disp"]
    body = window_shards if rows == 2 and mesh.shape["disp"] == 4 and pieces == 8 else shards
    return jax.shard_map(
        body,
        mesh=mesh,
        in_specs=(
            P(("tiles", "rows"), ("cols", "disp"), None),
            P(("tiles", "rows"), ("cols", "disp"), None),
            P(),
            P(),
            P(),
        ),
        out_specs=P(("tiles", "rows"), ("cols", "disp")),
        check_vma=False,
    )
```

```python
import functools

import jax
import jax.numpy as jnp
from jax import lax
from jax.experimental import pallas as pl
from jax.experimental.pallas import tpu as pltpu
from jax.sharding import PartitionSpec as P

MID = 2
DDEV = 16


def extended_2(block, sides, width):
    for axis, dim in sides:
        count = lax.axis_size(axis)
        forward = [(i, i + 1) for i in range(count - 1)]
        backward = [(target, source) for source, target in forward]
        low = lax.ppermute(
            lax.slice_in_dim(block, block.shape[dim] - width, None, axis=dim), axis, forward
        )
        high = lax.ppermute(lax.slice_in_dim(block, 0, width, axis=dim), axis, backward)
        block = jnp.concatenate([low, block, high], axis=dim)
    return block


def passed_along(x, axis, by):
    peers = lax.axis_size(axis)
    pairs = [(i, i + by) for i in range(peers) if 0 <= i + by < peers]
    return lax.ppermute(x, axis, pairs)


def combined_all(part, axis, combine):
    gathered = jax.tree.map(lambda a: lax.all_gather(a, axis), part)

    def take(source):
        return jax.tree.map(lambda a: lax.dynamic_index_in_dim(a, source, 0, False), gathered)

    return lax.fori_loop(
        1, lax.axis_size(axis), lambda source, state: combine(state, take(source)), take(0)
    )


def correlate(left_full, extended, groups, first_disp, count, total_disp):
    rows_here, width_here, channels = left_full.shape
    group_size = channels // groups
    left_groups = left_full.reshape(rows_here, width_here, groups, group_size)

    def single(offset):
        disp_value = first_disp + offset
        shifted = lax.dynamic_slice_in_dim(extended, 2 * width_here - disp_value, width_here, 1)
        right_groups = shifted.reshape(rows_here, width_here, groups, group_size)
        corr = (
            jnp.einsum(
                "hwgc,hwgc->ghw", left_groups, right_groups, preferred_element_type=jnp.float32
            )
            / group_size
        )
        inside = (disp_value >= 0) & (disp_value < total_disp)
        return jnp.where(inside, corr, 0.0).astype(jnp.bfloat16)

    return lax.map(single, jnp.arange(count, dtype=jnp.int32))


def convolve(padded, kernel):
    depth_out = padded.shape[0] - 2
    in_chans = padded.shape[1]
    rows_out = padded.shape[2] - 2
    cols_out = padded.shape[3] - 2
    out_chans = kernel.shape[1]
    columns = jnp.concatenate(
        [
            padded[:, :, row_tap : row_tap + rows_out, col_tap : col_tap + cols_out]
            for row_tap in range(3)
            for col_tap in range(3)
        ],
        axis=1,
    )
    flat = columns.reshape(depth_out + 2, 9 * in_chans, rows_out * cols_out)
    summed = jnp.zeros((depth_out, out_chans, rows_out * cols_out), jnp.float32)
    for disp_tap in range(3):
        taps = (
            jnp.transpose(kernel[9 * disp_tap : 9 * disp_tap + 9], (1, 0, 2))
            .reshape(out_chans, 9 * in_chans)
            .astype(flat.dtype)
        )
        summed = summed + jnp.einsum(
            "ok,dkn->don",
            taps,
            flat[disp_tap : disp_tap + depth_out],
            preferred_element_type=jnp.float32,
            precision=lax.Precision.HIGHEST,
        )
    return summed.reshape(depth_out, out_chans, rows_out, cols_out)


def widen(hidden):
    return extended_2(hidden, (("disp", 0), ("rows", 2), ("cols", 3)), 1)


def combine_parts(earlier, later):
    highest = jnp.maximum(earlier[0], later[0])
    scale_one = jnp.exp(earlier[0] - highest)
    scale_two = jnp.exp(later[0] - highest)
    return (
        highest,
        earlier[1] * scale_one + later[1] * scale_two,
        earlier[2] * scale_one + later[2] * scale_two,
    )


def shards(left_feat, right_feat, conv_first, conv_mid, conv_last):
    piece_width = left_feat.shape[1]
    groups = conv_first.shape[2]
    disp_count = lax.axis_size("disp")
    depth_here = DDEV
    total_disp = depth_here * disp_count
    first_disp = lax.axis_index("disp") * depth_here
    left_full, right_full = (
        lax.all_gather(left_feat, "disp", axis=1, tiled=True),
        lax.all_gather(right_feat, "disp", axis=1, tiled=True),
    )
    prior_full = passed_along(right_full, "cols", 1)
    extended = jnp.concatenate([jnp.zeros_like(right_full), prior_full, right_full], axis=1)
    volume = correlate(left_full, extended, groups, first_disp, depth_here, total_disp)
    padded = extended_2(volume, (("disp", 0), ("rows", 2), ("cols", 3)), 1)
    hidden = jax.nn.relu(convolve(padded, conv_first))
    for layer in range(MID):
        hidden = jax.nn.relu(convolve(widen(hidden), conv_mid[layer]))
    cost_cube = convolve(widen(hidden), conv_last)[:, 0]
    levels = (
        (first_disp + jnp.arange(depth_here, dtype=jnp.int32)).astype(jnp.float32) / total_disp
    )[:, None, None]
    local_high = jnp.max(cost_cube, axis=0)
    weights = jnp.exp(cost_cube - local_high[None])
    merged = combined_all(
        (local_high, jnp.sum(weights, axis=0), jnp.sum(weights * levels, axis=0)),
        "disp",
        combine_parts,
    )
    whole_row = merged[2] / merged[1]
    return lax.dynamic_slice_in_dim(whole_row, lax.axis_index("disp") * piece_width, piece_width, 1)


HALO = 4
GROUP = 4


EDGE = 16


def permutation(row, channels, groups):
    size = channels // groups
    lane = lax.broadcasted_iota(jnp.int32, (1, 128 * size), 1)
    group = lane % 64
    wanted = group * size + lane // 128
    wanted = jnp.where((group < groups) & ((lane // 64) % 2 == row), wanted, -1)
    channel = lax.broadcasted_iota(jnp.int32, (channels, 128 * size), 0)
    return (channel == wanted).astype(jnp.float32).astype(jnp.bfloat16)


def tap_of(a, r_in, r_out, e):
    return 9 * a + 3 * (r_in - r_out + 1) + e


def build_first(taps_ref, banded_ref):
    banded_ref[...] = jnp.zeros_like(banded_ref)
    outs, ins = taps_ref.shape[1:]
    blank = jnp.zeros((outs, 64 - ins), jnp.float32)
    for e in range(3):
        for r_out in range(2):
            for a in range(3):
                slabs = []
                for r_in in range(2):
                    slabs += [taps_ref[tap_of(a, r_in, r_out, e)].astype(jnp.float32), blank]
                block = jnp.concatenate(slabs, axis=1).astype(jnp.bfloat16)
                for d_out in range(GROUP):
                    at = e * 256 + d_out * 64 + r_out * 32
                    lane = 128 * (d_out + a)
                    banded_ref[at : at + outs, lane : lane + 128] = block


def build_mid(taps_ref, banded_ref):
    banded_ref[...] = jnp.zeros_like(banded_ref)
    outs = taps_ref.shape[1]
    blank = jnp.zeros((outs, 64), jnp.float32)
    for e in range(3):
        for r_out in range(2):
            slabs = [
                taps_ref[tap_of(a, r_in, r_out, e)].astype(jnp.float32)
                for a in range(3)
                for r_in in range(2)
            ]
            even = jnp.concatenate(slabs + [blank], axis=1).astype(jnp.bfloat16)
            odd = jnp.concatenate([blank] + slabs, axis=1).astype(jnp.bfloat16)
            for d_out in range(GROUP):
                at = e * 256 + d_out * 64 + r_out * 32
                block = even if d_out % 2 == 0 else odd
                for lane in (128 * (d_out // 2), 384 + 128 * (d_out // 2)):
                    banded_ref[at : at + outs, lane : lane + 256] = block


def build_last(taps_ref, banded_ref):
    banded_ref[...] = jnp.zeros_like(banded_ref)
    taps = taps_ref[...].astype(jnp.float32)
    for e in range(3):
        lines = []
        for d_out in range(GROUP):
            for r_out in range(2):
                parts = [
                    taps[tap_of(a, r_in, r_out, e) : tap_of(a, r_in, r_out, e) + 1]
                    for a in range(3)
                    for r_in in range(2)
                ]
                if d_out > 0:
                    parts.insert(0, jnp.zeros((1, 64 * d_out), jnp.float32))
                if d_out < GROUP - 1:
                    parts.append(jnp.zeros((1, 64 * (GROUP - 1 - d_out)), jnp.float32))
                lines.append(jnp.concatenate(parts, axis=1))
        lines.append(jnp.zeros((8, 384), jnp.float32))
        block = jnp.concatenate(lines, axis=0).astype(jnp.bfloat16)
        banded_ref[128 * e : 128 * e + 16, 0:384] = block
        banded_ref[128 * e : 128 * e + 16, 384:768] = block


def across(x, banded):
    return lax.dot_general(
        x, banded, (((1,), (1,)), ((), ())), preferred_element_type=jnp.float32
    )


def exchange_plan(width):
    right_at = width + 2 * EDGE
    own = right_at + EDGE + 2 * width
    copies = []
    for other in (1, 0):
        copies.append((1, 2, other, 0, own - 2 * width, width))
        copies.append((1, 3, other, width - EDGE, right_at, EDGE))
        copies.append((1, 1, other, 0, own - width, width))
        copies.append((1, -1, other, 0, own + width, EDGE))
        copies.append((0, 1, other, width - EDGE, 0, EDGE))
        copies.append((0, -1, other, 0, EDGE + width, EDGE))
    copies.append((1, 0, 1, 0, own, width))
    copies.append((0, 0, 1, 0, EDGE, width))
    return tuple(copies), own, own + width + EDGE


def exchange_steps(left_ref, right_ref, held, send_sem, recv_sem, own_sem):
    width = left_ref.shape[1]
    copies, own, _ = exchange_plan(width)
    row, col, disp = lax.axis_index("rows"), lax.axis_index("cols"), lax.axis_index("disp")
    col_disps = lax.axis_size("disp")
    pieces = col_disps * lax.axis_size("cols")
    piece = col * col_disps + disp
    barrier = pltpu.get_barrier_semaphore()

    def device(other, by):
        target = piece + by
        return {
            "tiles": lax.axis_index("tiles"),
            "disp": target % col_disps,
            "rows": (row + other) % 2,
            "cols": target // col_disps,
        }

    def exists(by):
        return (piece + by >= 0) & (piece + by < pieces)

    def copy(number):
        view, by, other, source, target, count = copies[number]
        return pltpu.make_async_remote_copy(
            src_ref=(left_ref if view == 0 else right_ref).at[0, pl.ds(source, count)],
            dst_ref=held.at[row, pl.ds(target, count)],
            send_sem=send_sem.at[number],
            recv_sem=recv_sem.at[number],
            device_id=device(other, by),
            device_id_type=pl.DeviceIdType.MESH,
        )

    def greet():
        held[...] = jnp.zeros_like(held)
        for by in range(-3, 4):
            for other in range(2):
                if by == 0 and other == 0:
                    continue

                @pl.when(exists(by))
                def _():
                    pl.semaphore_signal(
                        barrier,
                        inc=1,
                        device_id=device(other, by),
                        device_id_type=pl.DeviceIdType.MESH,
                    )

    def send():
        partners = jnp.int32(-1)
        for by in range(-3, 4):
            partners = partners + 2 * exists(by).astype(jnp.int32)
        pl.semaphore_wait(barrier, partners)
        for number in range(len(copies)):

            @pl.when(exists(copies[number][1]))
            def _():
                copy(number).start()

        for load in own_loads:
            load.start()

    own_loads = [
        pltpu.make_async_copy(
            source.at[0], held.at[row, pl.ds(target, width)], own_sem.at[number]
        )
        for number, (source, target) in enumerate(((left_ref, EDGE), (right_ref, own)))
    ]

    def receive():
        for load in own_loads:
            load.wait()
        for number in range(len(copies)):
            by = copies[number][1]

            @pl.when(exists(by))
            def _():
                copy(number).wait_send()

            @pl.when(exists(-by))
            def _():
                copy(number).wait_recv()

    return greet, send, receive


def whole_kernel(
    disps,
    width_all,
    left_ref,
    right_ref,
    first_hbm,
    mid_hbm,
    last_hbm,
    out_ref,
    feat_ref,
    send_sem,
    recv_sem,
    own_sem,
    load_sem,
    first_taps,
    mid_taps,
    last_taps,
    a_ref,
    p_ref,
    f_ref,
    first_ref,
    mid_ref,
    last_ref,
):
    width_here = out_ref.shape[1]
    wide = width_here + 2 * HALO
    span = disps + wide
    groups_d = disps // GROUP + 1
    rows = groups_d * wide
    greet, send, receive = exchange_steps(left_ref, right_ref, feat_ref, send_sem, recv_sem, own_sem)
    loads = [
        pltpu.make_async_copy(source, target, load_sem.at[number])
        for number, (source, target) in enumerate(
            ((first_hbm, first_taps), (mid_hbm, mid_taps), (last_hbm, last_taps))
        )
    ]
    greet()
    for load in loads:
        load.start()
    a_ref[...] = jnp.zeros_like(a_ref)
    send()
    loads[0].wait()
    build_first(first_taps, first_ref)
    loads[1].wait()
    for layer in range(MID):
        build_mid(mid_taps.at[layer], mid_ref.at[layer])
    loads[2].wait()
    build_last(last_taps, last_ref)
    receive()
    channels, groups = feat_ref.shape[2], first_taps.shape[2]
    f_ref[...] = jnp.dot(
        feat_ref[0], permutation(0, channels, groups), preferred_element_type=jnp.float32
    ) + jnp.dot(
        feat_ref[1], permutation(1, channels, groups), preferred_element_type=jnp.float32
    )
    left_at = EDGE - HALO
    right_at = width_here + 2 * EDGE + EDGE - HALO
    size = f_ref.shape[1] // 128
    for d in range(disps):
        acc = None
        for k in range(size):
            lanes = slice(128 * k, 128 * k + 128)
            start = right_at + disps - d
            term = f_ref[left_at : left_at + wide, lanes] * f_ref[start : start + wide, lanes]
            acc = term if acc is None else acc + term
        slab = (acc / size).astype(jnp.bfloat16)
        stored = d + HALO
        group, place = divmod(stored, GROUP)
        a_ref[group * wide : (group + 1) * wide, 128 * place : 128 * place + 128] = slab
        if place < 2 and group > 0:
            lane = 128 * (GROUP + place)
            a_ref[(group - 1) * wide : group * wide, lane : lane + 128] = slab

    piece = lax.axis_index("cols") * lax.axis_size("disp") + lax.axis_index("disp")
    column = piece * width_here - HALO + lax.broadcasted_iota(jnp.int32, (wide, 256), 0)
    in_image = (column >= 0) & (column < width_all)
    lane_disp = lax.broadcasted_iota(jnp.int32, (wide, 256), 1) // 64

    for layer in range(MID + 1):
        taps_ref = first_ref if layer == 0 else mid_ref.at[layer - 1]
        p_ref[8 : 8 + rows, :] = across(a_ref[...], taps_ref[...])
        base = layer + 1 - HALO
        for group in range(groups_d):
            at = 8 + group * wide
            total = (
                p_ref[at - 1 : at - 1 + wide, 0:256]
                + p_ref[at : at + wide, 256:512]
                + p_ref[at + 1 : at + 1 + wide, 512:768]
            )
            low = base + GROUP * group
            keep = in_image
            if low < 0 or low + GROUP > disps:
                keep = keep & (lane_disp >= -low) & (lane_disp < disps - low)
            total = jnp.where(keep, jnp.maximum(total, 0.0), 0.0)
            high = total.astype(jnp.bfloat16)
            rest = (total - high.astype(jnp.float32)).astype(jnp.bfloat16)
            here = slice(group * wide, (group + 1) * wide)
            a_ref[here, 0:256] = high
            a_ref[here, 384:640] = rest
            if group > 0:
                before = slice((group - 1) * wide, group * wide)
                a_ref[before, 256:384] = high[:, 0:128]
                a_ref[before, 640:768] = rest[:, 0:128]
            if group == groups_d - 1:
                a_ref[here, 256:384] = jnp.zeros((wide, 128), jnp.bfloat16)
                a_ref[here, 640:768] = jnp.zeros((wide, 128), jnp.bfloat16)

    used = (groups_d - 1) * wide
    p_ref[8 : 8 + used, 0:384] = across(a_ref[0:used], last_ref[...])
    costs = []
    for group in range(groups_d - 1):
        at = 8 + group * wide
        costs.append(
            p_ref[at - 1 : at - 1 + wide, 0:128]
            + p_ref[at : at + wide, 128:256]
            + p_ref[at + 1 : at + 1 + wide, 256:384]
        )
    lane = lax.broadcasted_iota(jnp.int32, (wide, 128), 1)
    mine = lane % 2 == lax.axis_index("rows")
    mine = mine & (lane < 2 * GROUP)
    top = functools.reduce(jnp.maximum, costs)
    top = jnp.max(jnp.where(mine, top, -jnp.inf), axis=1, keepdims=True)
    weight_sum = jnp.zeros((wide, 128), jnp.float32)
    level_sum = jnp.zeros((wide, 128), jnp.float32)
    for group, cost in enumerate(costs):
        weight = jnp.where(mine, jnp.exp(jnp.where(mine, cost - top, 0.0)), 0.0)
        level = (lane // 2 + GROUP * group).astype(jnp.float32) * (1.0 / disps)
        weight_sum += weight
        level_sum += weight * level
    estimate = jnp.sum(level_sum, axis=1, keepdims=True) / jnp.sum(
        weight_sum, axis=1, keepdims=True
    )
    place = lax.broadcasted_iota(jnp.int32, (wide, 128), 0)
    line = jnp.sum(jnp.where(place == lane + HALO, estimate, 0.0), axis=0, keepdims=True)
    out_ref[...] = line[:, 0:width_here]


def window_shards(left_feat, right_feat, conv_first, conv_mid, conv_last):
    width = left_feat.shape[1]
    channels = left_feat.shape[2]
    groups = conv_first.shape[2]
    disps = DDEV * lax.axis_size("disp")
    width_all = width * lax.axis_size("disp") * lax.axis_size("cols")
    copies, _, held_rows = exchange_plan(width)
    wide = width + 2 * HALO
    rows = (disps // GROUP + 1) * wide
    return pl.pallas_call(
        functools.partial(whole_kernel, disps, width_all),
        out_shape=jax.ShapeDtypeStruct((1, width), jnp.float32),
        in_specs=[pl.BlockSpec(memory_space=pltpu.HBM)] * 5,
        out_specs=pl.BlockSpec(memory_space=pltpu.VMEM),
        scratch_shapes=[
            pltpu.VMEM((2, held_rows, channels), jnp.bfloat16),
            pltpu.SemaphoreType.DMA((len(copies),)),
            pltpu.SemaphoreType.DMA((len(copies),)),
            pltpu.SemaphoreType.DMA((2,)),
            pltpu.SemaphoreType.DMA((3,)),
            pltpu.VMEM(conv_first.shape, jnp.bfloat16),
            pltpu.VMEM(conv_mid.shape, jnp.bfloat16),
            pltpu.VMEM((27, conv_last.shape[2]), jnp.bfloat16),
            pltpu.VMEM((rows, 768), jnp.bfloat16),
            pltpu.VMEM((rows + 16, 768), jnp.float32),
            pltpu.VMEM((held_rows, (channels // groups) * 128), jnp.float32),
            pltpu.VMEM((768, 768), jnp.bfloat16),
            pltpu.VMEM((MID, 768, 768), jnp.bfloat16),
            pltpu.VMEM((384, 768), jnp.bfloat16),
        ],
        compiler_params=pltpu.CompilerParams(
            vmem_limit_bytes=56 * 1024 * 1024, collective_id=0, has_side_effects=True
        ),
    )(left_feat, right_feat, conv_first, conv_mid, conv_last.reshape(27, -1))


def solution(mesh):
    rows, pieces = mesh.shape["rows"], mesh.shape["cols"] * mesh.shape["disp"]
    body = window_shards if rows == 2 and mesh.shape["disp"] == 4 and pieces == 8 else shards
    return jax.shard_map(
        body,
        mesh=mesh,
        in_specs=(
            P(("tiles", "rows"), ("cols", "disp"), None),
            P(("tiles", "rows"), ("cols", "disp"), None),
            P(),
            P(),
            P(),
        ),
        out_specs=P(("tiles", "rows"), ("cols", "disp")),
        check_vma=False,
    )
```
